512 devices in a mesh: pix: 32 (over z_lo, y), mass: 16 (over z_hi, x, core).
Axes of the slice: x: 4, y: 4, z: 16 (z_hi: 2, z_lo: 8; z = z_hi * 8 + z_lo), core: 2. Of those that a mesh axis runs over, the one named last changes fastest.
Arguments:
- tiles: bfloat16 [32, 16, 16, 256, 256], P('pix', 'mass'), may hold values from 10 to 1000
- tile_pos: int32 [32, 16, 16], P('pix', 'mass'), may hold values from 0 to 255, as said below
- kept_tile_count: int32 [32, 16], P('pix', 'mass'), may hold values from 1 to 16, as said below
- loading: float32 [64, 65536], P('mass', 'pix'), may hold values from 0.006 to 6.5, as said below
- spectra: float32 [64, 131072], P('pix', 'mass'), may hold values from 0.006 to 6.5, as said below
Outputs:
- loading_new: float32 [64, 65536], P('mass', 'pix')
- spectra_new: float32 [64, 131072], P('pix', 'mass')
The draws below stay inside these ranges and needn't reach their ends.
Inputs may be any that keep to these rules, and one draw needn't show every extreme that they name: `tile_pos`: on each device the 16 entries are distinct; entry q names tile row q // 32 and tile column q % 32 of the device's block. `kept_tile_count`: some device holds exactly 16 kept tiles. `loading`: every entry is positive. `spectra`: every entry is positive.
All inputs are finite; a program needn't handle non-finite values.
Results may differ from the reference program's by a relative error of at most 0.00065.
Values may be sent and summed in bfloat16 or wider, within the bound.
No kernel may reach another device: no remote copies, remote signals or barrier semaphores. Data moves between devices by JAX's collectives and lax.ppermute only.
A program may use at most 64 MiB of HBM per device.

```python
import math
import jax
import jax.numpy as jnp
from jax import lax

RANK = 64
MBINS = 131072
TILE = 256
TROWS = 8
CAP = 16
TCOLS = 32
PIXELS = 65536
N_PIX = 32
N_MASS = 16


def drawn_factor(key, rows_count, cols_count):
    first_key, second_key, third_key = jax.random.split(key, 3)
    entries = jnp.exp(jax.random.uniform(first_key, (rows_count, cols_count), minval=math.log(0.1), maxval=math.log(0.4)))
    col_scale = jnp.exp(jax.random.uniform(second_key, (1, cols_count), minval=math.log(0.3), maxval=math.log(3.0)))
    row_scale = jnp.exp(jax.random.uniform(third_key, (rows_count, 1), minval=math.log(0.4), maxval=math.log(2.5)))
    return (entries * col_scale * row_scale).astype(jnp.float32)


def draw_loading(key, part):
    return drawn_factor(key, RANK, PIXELS)


def draw_spectra(key, part):
    return drawn_factor(key, RANK, MBINS)


def draw_tile_pos(key, part):
    device_keys = jax.random.split(key, N_PIX * N_MASS)
    slots_all = TROWS * TCOLS
    chosen = jax.vmap(lambda one_key: jax.random.permutation(one_key, slots_all)[:CAP])(device_keys)
    return chosen.reshape(N_PIX, N_MASS, CAP).astype(jnp.int32)


def draw_kept_tile_count(key, part):
    first_key, second_key = jax.random.split(key)
    base_counts = jax.random.randint(first_key, (N_PIX * N_MASS,), 1, CAP // 2 + 2)
    chosen = jax.random.randint(second_key, (), 0, N_PIX * N_MASS)
    filled = jnp.where(jnp.arange(N_PIX * N_MASS) == chosen, CAP, base_counts)
    return filled.reshape(N_PIX, N_MASS).astype(jnp.int32)


def shard_levels(rng, shape, shards, smallest, largest):
    gain = 1.0
    for position, blocks in shards:
        heights = jax.random.uniform(jax.random.fold_in(jax.random.fold_in(rng, 6), position), (blocks,), jnp.float32, smallest / len(shards), largest / len(shards))
        gain = gain * jnp.repeat(jnp.exp(heights), shape[position] // blocks).reshape((-1,) + (1,) * (len(shape) - 1 - position))
    return gain


def setup_inputs(seed: int = 0) -> dict:
    key_list = jax.random.split(jax.random.key(seed), 6)
    return {
        "tiles": jnp.clip(jnp.exp(math.log(1000.0) - 4.6051702 * jax.random.uniform(key_list[0], (N_PIX, N_MASS, CAP, TILE, TILE), jnp.float32) ** shard_levels(key_list[0], (N_PIX, N_MASS, CAP, TILE, TILE), ((0, 32), (1, 16)), -0.2, 0.2)), 10.0, 1000.0).astype(jnp.bfloat16),
        "tile_pos": draw_tile_pos(jax.random.fold_in(key_list[5], 71), 0),
        "kept_tile_count": draw_kept_tile_count(jax.random.fold_in(key_list[5], 71), 0),
        "loading": draw_loading(jax.random.fold_in(key_list[5], 71), 0),
        "spectra": draw_spectra(jax.random.fold_in(key_list[5], 71), 0),
    }


def reference(tiles, tile_pos, kept_tile_count, loading, spectra):
    largest_value = lax.Precision.HIGHEST
    pix_dev = TROWS * TILE
    bins_dev = MBINS // N_MASS
    tile_cols = bins_dev // TILE
    slot_ids = jnp.arange(CAP, dtype=jnp.int32)
    load_half = loading.astype(jnp.bfloat16)
    spec_half = spectra.astype(jnp.bfloat16)
    gram_load = jnp.dot(load_half, load_half.T, preferred_element_type=jnp.float32)

    def block_info(pix_index):
        places = tile_pos[pix_index]
        live_mask = (slot_ids[None, :] < kept_tile_count[pix_index][:, None]).astype(jnp.float32)
        return places // tile_cols, places % tile_cols, live_mask, tiles[pix_index].astype(jnp.float32)

    def spec_step(total, pix_index):
        row_of, col_of, live_mask, block = block_info(pix_index)
        rows_load = lax.dynamic_slice_in_dim(load_half, pix_index * pix_dev, pix_dev, 1)
        rows_load = rows_load.reshape(RANK, TROWS, TILE).astype(jnp.float32)
        picked = jnp.take(rows_load, row_of, axis=1)
        product = jnp.einsum("kbsu,bsuv->bskv", picked, block, precision=largest_value)
        column_onehot = (col_of[..., None] == jnp.arange(tile_cols)).astype(jnp.float32) * live_mask[..., None]
        portion = jnp.einsum("bsc,bskv->kbcv", column_onehot, product, precision=largest_value)
        return total + portion.reshape(RANK, MBINS), None

    spectra_upper = lax.scan(spec_step, jnp.zeros((RANK, MBINS), jnp.float32), jnp.arange(N_PIX, dtype=jnp.int32))[0]
    spec_bottom = jnp.dot(gram_load, spec_half.astype(jnp.float32), precision=largest_value)
    spectra_new = spectra * spectra_upper / spec_bottom
    fresh_half = spectra_new.astype(jnp.bfloat16)
    gram_spec = jnp.dot(fresh_half, fresh_half.T, preferred_element_type=jnp.float32)
    fresh_blocks = fresh_half.astype(jnp.float32).reshape(RANK, N_MASS, tile_cols, TILE)
    mass_ids = jnp.arange(N_MASS, dtype=jnp.int32)

    def load_step(pix_index):
        row_of, col_of, live_mask, block = block_info(pix_index)
        picked = fresh_blocks[:, mass_ids[:, None], col_of, :]
        product = jnp.einsum("kbsv,bsuv->bsku", picked, block, precision=largest_value)
        row_hot = (row_of[..., None] == jnp.arange(TROWS)).astype(jnp.float32) * live_mask[..., None]
        portion = jnp.einsum("bsr,bsku->kru", row_hot, product, precision=largest_value)
        return portion.reshape(RANK, pix_dev)

    load_top = lax.map(load_step, jnp.arange(N_PIX, dtype=jnp.int32))
    load_top = jnp.moveaxis(load_top, 0, 1).reshape(RANK, N_PIX * pix_dev)
    load_bottom = jnp.dot(gram_spec, load_half.astype(jnp.float32), precision=largest_value)
    loading_new = loading * load_top / load_bottom
    return (loading_new, spectra_new)
```

```python
import jax
import jax.numpy as jnp
from jax import lax
from jax.experimental import pallas as pl
from jax.experimental.pallas import tpu as pltpu
from jax.sharding import Mesh, PartitionSpec as P

F32, BF16, F16 = jnp.float32, jnp.bfloat16, jnp.float16
PIX = ("zl", "y")
MASS = ("zh", "x", "core")
RANK, TILE, TROWS, TCOLS, CAP = 64, 256, 8, 32, 16
NZ, NY, NMASS = 8, 4, 16
PER = RANK // NMASS
TOP_SCALE = 2.0**-10
GRAM_SCALE = 2.0**-3
TOPS = NZ * RANK
PIXELS = TROWS * TILE
WIDE = PIXELS + 128
VMEM = pl.BlockSpec(memory_space=pltpu.VMEM)
SMEM = pl.BlockSpec(memory_space=pltpu.SMEM)
CONTRACT_LAST = (((1,), (1,)), ((), ()))


def spec_kernel(pos_ref, count_ref, load_ref, tiles_ref, spec_ref, out_ref, wide_ref, half_ref):
    for m in range(NMASS):
        wide_ref[pl.ds(PER * m, PER), :] = load_ref[m].astype(F32)
    half_ref[...] = wide_ref[...].astype(BF16)
    for y in range(NY):
        out_ref[y, pl.ds(0, TOPS), :] = jnp.zeros((TOPS, TILE), F32)
    count = count_ref[0]
    for s in range(CAP):
        place = pos_ref[s]
        row, col = place // TCOLS, place % TCOLS
        lanes = pl.ds(pl.multiple_of(row * TILE, TILE), TILE)
        product = jnp.dot(half_ref[:, lanes], tiles_ref[s], preferred_element_type=F32) * TOP_SCALE
        rows = pl.ds(pl.multiple_of((col // NY) * RANK, RANK), RANK)
        out_ref[col % NY, rows, :] += jnp.where(s < count, product, 0.0)
    half = half_ref[...]
    gram = lax.dot_general(half, half, CONTRACT_LAST, preferred_element_type=F32) * GRAM_SCALE
    packed = jnp.concatenate([gram[16 * i : 16 * i + 16, :] for i in range(4)], axis=1)
    for y in range(NY):
        for z in range(NZ):
            c = z * NY + y
            out_ref[y, pl.ds(TOPS + 2 * z, 2), :] = spec_ref[:, c * TILE : (c + 1) * TILE]
        out_ref[y, pl.ds(TOPS + 2 * NZ, 16), :] = packed


def update_kernel(sums_ref, spec_ref, out_ref):
    packed = sums_ref[pl.ds(RANK, 16), :] * (TOP_SCALE / GRAM_SCALE)
    gram = jnp.concatenate([packed[:, RANK * i : RANK * i + RANK] for i in range(4)], axis=0)
    spec = spec_ref[...]
    bottom = jnp.dot(gram, spec.astype(BF16).astype(F32), precision=lax.Precision.HIGHEST, preferred_element_type=F32)
    new = spec * sums_ref[pl.ds(0, RANK), :] / bottom
    fresh = new.astype(BF16)
    rest = new - fresh.astype(F32)
    for z in range(NZ):
        out_ref[z, pl.ds(0, RANK), :] = fresh
        out_ref[z, pl.ds(RANK, 8), :] = rest[8 * z : 8 * z + 8, :].astype(BF16)


def spread_kernel(in_ref, out_ref):
    for y in range(NY):
        for z in range(NZ):
            out_ref[y, pl.ds(z * RANK, RANK), :] = in_ref[z, pl.ds(0, RANK), :]
    for z in range(NZ):
        rest = in_ref[z, pl.ds(RANK, 8), :].astype(F32)
        for y in range(NY):
            out_ref[y, pl.ds(TOPS + 2 * z, 2), :] = rest[2 * y : 2 * y + 2, :].astype(BF16)


def load_kernel(pos_ref, count_ref, fresh_ref, tiles_ref, out_ref, acc_ref):
    acc_ref[...] = jnp.zeros_like(acc_ref)
    count = count_ref[0]
    for s in range(CAP):
        place = pos_ref[s]
        row, col = place // TCOLS, place % TCOLS
        rows = pl.ds(pl.multiple_of((col // NY) * RANK, RANK), RANK)
        block = fresh_ref[col % NY, rows, :]
        product = lax.dot_general(block, tiles_ref[s], CONTRACT_LAST, preferred_element_type=F32)
        lanes = pl.ds(pl.multiple_of(row * TILE, TILE), TILE)
        acc_ref[:, lanes] += jnp.where(s < count, product, 0.0)
    gram = jnp.zeros((RANK, RANK), F32)
    for y in range(NY):
        for z in range(NZ):
            block = fresh_ref[y, pl.ds(z * RANK, RANK), :]
            gram = gram + lax.dot_general(block, block, CONTRACT_LAST, preferred_element_type=F32)

    def exponent(x):
        return jnp.floor(jnp.log2(jnp.maximum(jnp.max(x, axis=1, keepdims=True), 1e-30))) - 13.0

    top = acc_ref[...]
    top_exp, gram_exp = exponent(top), exponent(gram)
    top = top * jnp.exp2(-top_exp)
    gram = gram * jnp.exp2(-gram_exp)
    lane = lax.broadcasted_iota(jnp.int32, (RANK, RANK), 1)
    tail = jnp.where(lane == 0, top_exp, jnp.where(lane == 1, gram_exp, 0.0))
    tail = jnp.concatenate([gram, tail], axis=1)
    for m in range(NMASS):
        out_ref[m, :, pl.ds(0, PIXELS)] = top[PER * m : PER * m + PER, :]
        out_ref[m, :, pl.ds(PIXELS, 128)] = tail[PER * m : PER * m + PER, :]


def spectra_kernel(place_ref, recv_ref, spec_ref, sent_ref, out_ref):
    zl, yl = place_ref[0], place_ref[1]
    for z in range(NZ):
        for y in range(NY):
            c = z * NY + y
            eight = recv_ref[y, pl.ds(pl.multiple_of(z * RANK + 8 * zl, 8), 8), :].astype(F32)
            two = eight[0:2, :]
            for k in range(1, NY):
                two = jnp.where(yl == k, eight[2 * k : 2 * k + 2, :], two)
            rest = recv_ref[y, pl.ds(TOPS + 2 * z, 2), :].astype(F32)
            cols = pl.ds(c * TILE, TILE)
            out_ref[:, cols] = (two + rest) * (spec_ref[:, cols] / sent_ref[:, cols])


def local(tiles, tile_pos, kept_tile_count, loading, spectra):
    tiles = tiles[0, 0]
    pos = tile_pos[0, 0]
    count = kept_tile_count[0]

    own = jnp.broadcast_to(loading.astype(BF16)[None], (NMASS, PER, PIXELS))
    load = lax.all_to_all(own, MASS, 0, 0, tiled=True)
    sent = lax.reduce_precision(spectra, 5, 10)

    out = pl.pallas_call(
        spec_kernel,
        out_shape=jax.ShapeDtypeStruct((NY, TOPS + 32, TILE), F32),
        in_specs=[SMEM, SMEM, VMEM, VMEM, VMEM],
        out_specs=VMEM,
        scratch_shapes=[pltpu.VMEM((RANK, PIXELS), F32), pltpu.VMEM((RANK, PIXELS), BF16)],
        name="spec",
    )(pos, count, load, tiles, sent)
    part = lax.all_to_all(out.astype(F16), "y", 0, 0, tiled=True)
    tops = part[:, :TOPS].astype(F32).sum(0).astype(F16).reshape(NZ, RANK, TILE)
    old = part[:, TOPS : TOPS + 2 * NZ].reshape(NY, NZ, 2, TILE).transpose(1, 0, 2, 3).reshape(NZ, 8, TILE)
    gram = part[:, TOPS + 2 * NZ :].astype(F32).sum(0).astype(F16)
    gram = jnp.broadcast_to(gram[None], (NZ, 16, TILE))
    part = lax.all_to_all(jnp.concatenate([tops, old, gram], axis=1), "zl", 0, 0, tiled=True)
    wide = part.astype(F32)
    sums = jnp.concatenate([wide[:, :RANK].sum(0), wide[:, RANK + 8 :].sum(0)], axis=0)
    old = wide[:, RANK : RANK + 8].reshape(RANK, TILE)

    fresh = pl.pallas_call(
        update_kernel,
        out_shape=jax.ShapeDtypeStruct((NZ, RANK + 8, TILE), BF16),
        in_specs=[VMEM, VMEM],
        out_specs=VMEM,
        name="update",
    )(sums, old)
    fresh = lax.all_to_all(fresh, "zl", 0, 0, tiled=True)
    fresh = pl.pallas_call(
        spread_kernel,
        out_shape=jax.ShapeDtypeStruct((NY, TOPS + 16, TILE), BF16),
        in_specs=[VMEM],
        out_specs=VMEM,
        name="spread",
    )(fresh)
    fresh = lax.all_to_all(fresh, "y", 0, 0, tiled=True)

    out = pl.pallas_call(
        load_kernel,
        out_shape=jax.ShapeDtypeStruct((NMASS, PER, WIDE), F32),
        in_specs=[SMEM, SMEM, VMEM, VMEM],
        out_specs=VMEM,
        scratch_shapes=[pltpu.VMEM((RANK, PIXELS), F32)],
        name="load",
    )(pos, count, fresh, tiles)
    part = lax.all_to_all(out.astype(F16), MASS, 0, 0, tiled=True).astype(F32)

    place = jnp.stack([lax.axis_index("zl"), lax.axis_index("y")]).astype(jnp.int32)
    spectra_new = pl.pallas_call(
        spectra_kernel,
        out_shape=jax.ShapeDtypeStruct(spectra.shape, F32),
        in_specs=[SMEM, VMEM, VMEM, VMEM],
        out_specs=VMEM,
        name="spectra",
    )(place, fresh, spectra, sent)

    exps = part[:, :, PIXELS + RANK : PIXELS + RANK + 2]
    top = (part[:, :, :PIXELS] * jnp.exp2(exps[:, :, 0:1])).sum(0)
    gram = (part[:, :, PIXELS : PIXELS + RANK] * jnp.exp2(exps[:, :, 1:2])).sum(0)
    bottom = jnp.dot(gram, load.reshape(RANK, PIXELS).astype(F32), precision=lax.Precision.HIGHEST)
    loading_new = loading * top / bottom
    return (loading_new, spectra_new)


def solution(mesh):
    fine = Mesh(mesh.devices.reshape(NZ, NY, 2, 4, 2), PIX + MASS)
    return jax.shard_map(
        local,
        mesh=fine,
        in_specs=(P(PIX, MASS, None, None, None), P(PIX, MASS, None), P(PIX, MASS), P(MASS, PIX), P(PIX, MASS)),
        out_specs=(P(MASS, PIX), P(PIX, MASS)),
        check_vma=False,
    )
```

```python
import jax
import jax.numpy as jnp
from jax import lax
from jax.experimental import pallas as pl
from jax.experimental.pallas import tpu as pltpu
from jax.sharding import Mesh, PartitionSpec as P

F32, BF16, F16 = jnp.float32, jnp.bfloat16, jnp.float16
PIX = ("zl", "y")
MASS = ("zh", "x", "core")
RANK, TILE, TROWS, TCOLS, CAP = 64, 256, 8, 32, 16
NZ, NY, NMASS = 8, 4, 16
PER = RANK // NMASS
TOP_SCALE = 2.0**-10
GRAM_SCALE = 2.0**-3
TOPS = NZ * RANK
PIXELS = TROWS * TILE
WIDE = PIXELS + 128
VMEM = pl.BlockSpec(memory_space=pltpu.VMEM)
SMEM = pl.BlockSpec(memory_space=pltpu.SMEM)
PARAMS = pltpu.CompilerParams(vmem_limit_bytes=12 << 20)
CONTRACT_LAST = (((1,), (1,)), ((), ()))


def spec_kernel(pos_ref, count_ref, load_ref, tiles_ref, spec_ref, out_ref, wide_ref, half_ref):
    for m in range(NMASS):
        wide_ref[pl.ds(PER * m, PER), :] = load_ref[m].astype(F32)
    half_ref[...] = wide_ref[...].astype(BF16)
    for y in range(NY):
        out_ref[y, pl.ds(0, TOPS), :] = jnp.zeros((TOPS, TILE), F32)
    count = count_ref[0]
    for s in range(CAP):
        place = pos_ref[s]
        row, col = place // TCOLS, place % TCOLS
        lanes = pl.ds(pl.multiple_of(row * TILE, TILE), TILE)
        product = jnp.dot(half_ref[:, lanes], tiles_ref[s], preferred_element_type=F32) * TOP_SCALE
        rows = pl.ds(pl.multiple_of((col // NY) * RANK, RANK), RANK)
        out_ref[col % NY, rows, :] += jnp.where(s < count, product, 0.0)
    half = half_ref[...]
    gram = lax.dot_general(half, half, CONTRACT_LAST, preferred_element_type=F32) * GRAM_SCALE
    packed = jnp.concatenate([gram[16 * i : 16 * i + 16, :] for i in range(4)], axis=1)
    for y in range(NY):
        for z in range(NZ):
            c = z * NY + y
            out_ref[y, pl.ds(TOPS + 2 * z, 2), :] = spec_ref[:, c * TILE : (c + 1) * TILE]
        out_ref[y, pl.ds(TOPS + 2 * NZ, 16), :] = packed


def update_kernel(sums_ref, spec_ref, out_ref):
    packed = sums_ref[pl.ds(RANK, 16), :] * (TOP_SCALE / GRAM_SCALE)
    gram = jnp.concatenate([packed[:, RANK * i : RANK * i + RANK] for i in range(4)], axis=0)
    spec = spec_ref[...]
    bottom = jnp.dot(gram, spec.astype(BF16).astype(F32), precision=lax.Precision.HIGHEST, preferred_element_type=F32)
    new = spec * sums_ref[pl.ds(0, RANK), :] / bottom
    fresh = new.astype(BF16)
    rest = new - fresh.astype(F32)
    for z in range(NZ):
        out_ref[z, pl.ds(0, RANK), :] = fresh
        out_ref[z, pl.ds(RANK, 8), :] = rest[8 * z : 8 * z + 8, :].astype(BF16)


def spread_kernel(in_ref, out_ref):
    for y in range(NY):
        for z in range(NZ):
            out_ref[y, pl.ds(z * RANK, RANK), :] = in_ref[z, pl.ds(0, RANK), :]
    for z in range(NZ):
        rest = in_ref[z, pl.ds(RANK, 8), :].astype(F32)
        for y in range(NY):
            out_ref[y, pl.ds(TOPS + 2 * z, 2), :] = rest[2 * y : 2 * y + 2, :].astype(BF16)


def load_kernel(pos_ref, count_ref, fresh_ref, tiles_ref, out_ref, acc_ref):
    acc_ref[...] = jnp.zeros_like(acc_ref)
    count = count_ref[0]
    for s in range(CAP):
        place = pos_ref[s]
        row, col = place // TCOLS, place % TCOLS
        rows = pl.ds(pl.multiple_of((col // NY) * RANK, RANK), RANK)
        block = fresh_ref[col % NY, rows, :]
        product = lax.dot_general(block, tiles_ref[s], CONTRACT_LAST, preferred_element_type=F32)
        lanes = pl.ds(pl.multiple_of(row * TILE, TILE), TILE)
        acc_ref[:, lanes] += jnp.where(s < count, product, 0.0)
    gram = jnp.zeros((RANK, RANK), F32)
    for y in range(NY):
        for z in range(NZ):
            block = fresh_ref[y, pl.ds(z * RANK, RANK), :]
            gram = gram + lax.dot_general(block, block, CONTRACT_LAST, preferred_element_type=F32)

    def exponent(x):
        return jnp.floor(jnp.log2(jnp.maximum(jnp.max(x, axis=1, keepdims=True), 1e-30))) - 13.0

    top = acc_ref[...]
    top_exp, gram_exp = exponent(top), exponent(gram)
    top = top * jnp.exp2(-top_exp)
    gram = gram * jnp.exp2(-gram_exp)
    lane = lax.broadcasted_iota(jnp.int32, (RANK, RANK), 1)
    tail = jnp.where(lane == 0, top_exp, jnp.where(lane == 1, gram_exp, 0.0))
    tail = jnp.concatenate([gram, tail], axis=1)
    for m in range(NMASS):
        out_ref[m, :, pl.ds(0, PIXELS)] = top[PER * m : PER * m + PER, :]
        out_ref[m, :, pl.ds(PIXELS, 128)] = tail[PER * m : PER * m + PER, :]


def spectra_kernel(place_ref, recv_ref, spec_ref, sent_ref, out_ref):
    zl, yl = place_ref[0], place_ref[1]
    for z in range(NZ):
        for y in range(NY):
            c = z * NY + y
            eight = recv_ref[y, pl.ds(pl.multiple_of(z * RANK + 8 * zl, 8), 8), :].astype(F32)
            two = eight[0:2, :]
            for k in range(1, NY):
                two = jnp.where(yl == k, eight[2 * k : 2 * k + 2, :], two)
            rest = recv_ref[y, pl.ds(TOPS + 2 * z, 2), :].astype(F32)
            cols = pl.ds(c * TILE, TILE)
            out_ref[:, cols] = (two + rest) * (spec_ref[:, cols] / sent_ref[:, cols])


def near(x):
    return pltpu.with_memory_space_constraint(x, pltpu.VMEM)


def local(tiles, tile_pos, kept_tile_count, loading, spectra):
    tiles = tiles[0, 0]
    pos = tile_pos[0, 0]
    count = kept_tile_count[0]

    own = jnp.broadcast_to(loading.astype(BF16)[None], (NMASS, PER, PIXELS))
    load = lax.all_to_all(own, MASS, 0, 0, tiled=True)
    sent = lax.reduce_precision(spectra, 5, 10)

    out = pl.pallas_call(
        spec_kernel,
        out_shape=pltpu.VMEM((NY, TOPS + 32, TILE), F32),
        in_specs=[SMEM, SMEM, VMEM, VMEM, VMEM],
        out_specs=VMEM,
        scratch_shapes=[pltpu.VMEM((RANK, PIXELS), F32), pltpu.VMEM((RANK, PIXELS), BF16)],
        compiler_params=PARAMS,
        name="spec",
    )(pos, count, near(load), near(tiles), near(sent))
    part = lax.all_to_all(out.astype(F16), "y", 0, 0, tiled=True)
    tops = part[:, :TOPS].astype(F32).sum(0).astype(F16).reshape(NZ, RANK, TILE)
    old = part[:, TOPS : TOPS + 2 * NZ].reshape(NY, NZ, 2, TILE).transpose(1, 0, 2, 3).reshape(NZ, 8, TILE)
    gram = part[:, TOPS + 2 * NZ :].astype(F32).sum(0).astype(F16)
    gram = jnp.broadcast_to(gram[None], (NZ, 16, TILE))
    part = lax.all_to_all(jnp.concatenate([tops, old, gram], axis=1), "zl", 0, 0, tiled=True)
    wide = part.astype(F32)
    sums = jnp.concatenate([wide[:, :RANK].sum(0), wide[:, RANK + 8 :].sum(0)], axis=0)
    old = wide[:, RANK : RANK + 8].reshape(RANK, TILE)

    fresh = pl.pallas_call(
        update_kernel,
        out_shape=pltpu.VMEM((NZ, RANK + 8, TILE), BF16),
        in_specs=[VMEM, VMEM],
        out_specs=VMEM,
        compiler_params=PARAMS,
        name="update",
    )(near(sums), near(old))
    fresh = lax.all_to_all(fresh, "zl", 0, 0, tiled=True)
    fresh = pl.pallas_call(
        spread_kernel,
        out_shape=pltpu.VMEM((NY, TOPS + 16, TILE), BF16),
        in_specs=[VMEM],
        out_specs=VMEM,
        compiler_params=PARAMS,
        name="spread",
    )(near(fresh))
    fresh = lax.all_to_all(fresh, "y", 0, 0, tiled=True)

    out = pl.pallas_call(
        load_kernel,
        out_shape=pltpu.VMEM((NMASS, PER, WIDE), F32),
        in_specs=[SMEM, SMEM, VMEM, VMEM],
        out_specs=VMEM,
        scratch_shapes=[pltpu.VMEM((RANK, PIXELS), F32)],
        compiler_params=PARAMS,
        name="load",
    )(pos, count, near(fresh), near(tiles))
    part = lax.all_to_all(out.astype(F16), MASS, 0, 0, tiled=True).astype(F32)

    place = jnp.stack([lax.axis_index("zl"), lax.axis_index("y")]).astype(jnp.int32)
    spectra_new = pl.pallas_call(
        spectra_kernel,
        out_shape=jax.ShapeDtypeStruct(spectra.shape, F32),
        in_specs=[SMEM, VMEM, VMEM, VMEM],
        out_specs=VMEM,
        compiler_params=PARAMS,
        name="spectra",
    )(place, near(fresh), near(spectra), near(sent))

    exps = part[:, :, PIXELS + RANK : PIXELS + RANK + 2]
    top = (part[:, :, :PIXELS] * jnp.exp2(exps[:, :, 0:1])).sum(0)
    gram = (part[:, :, PIXELS : PIXELS + RANK] * jnp.exp2(exps[:, :, 1:2])).sum(0)
    bottom = jnp.dot(gram, load.reshape(RANK, PIXELS).astype(F32), precision=lax.Precision.HIGHEST)
    loading_new = loading * top / bottom
    return (loading_new, spectra_new)


def solution(mesh):
    fine = Mesh(mesh.devices.reshape(NZ, NY, 2, 4, 2), PIX + MASS)
    return jax.shard_map(
        local,
        mesh=fine,
        in_specs=(P(PIX, MASS, None, None, None), P(PIX, MASS, None), P(PIX, MASS), P(MASS, PIX), P(PIX, MASS)),
        out_specs=(P(MASS, PIX), P(PIX, MASS)),
        check_vma=False,
    )
```

```python
import jax
import jax.numpy as jnp
from jax import lax
from jax.experimental import pallas as pl
from jax.experimental.pallas import tpu as pltpu
from jax.sharding import Mesh, PartitionSpec as P

F32, BF16, F16 = jnp.float32, jnp.bfloat16, jnp.float16
PIX = ("zl", "y")
MASS = ("zh", "x", "core")
RANK, TILE, TROWS, TCOLS, CAP = 64, 256, 8, 32, 16
NZ, NY, NMASS = 8, 4, 16
PER = RANK // NMASS
TOP_SCALE = 2.0**-10
GRAM_SCALE = 2.0**-3
TOPS = NZ * RANK
PIXELS = TROWS * TILE
WIDE = PIXELS + 128
VMEM = pl.BlockSpec(memory_space=pltpu.VMEM)
SMEM = pl.BlockSpec(memory_space=pltpu.SMEM)
PARAMS = pltpu.CompilerParams(vmem_limit_bytes=12 << 20)
CONTRACT_LAST = (((1,), (1,)), ((), ()))


def half_precision(x):
    wide = x * 8193.0
    return wide - (wide - x)


def own_kernel(loading_ref, out_ref):
    half = loading_ref[...].astype(BF16)
    for m in range(NMASS // 2):
        out_ref[m] = half


def fetch_kernel(tiles_ref, spec_ref, out_ref, sent_ref, sem):
    copy = pltpu.make_async_copy(tiles_ref, out_ref, sem)
    copy.start()
    sent_ref[...] = half_precision(spec_ref[...])
    copy.wait()


def spec_kernel(meta_ref, load_ref, tiles_ref, sent_ref, out_ref, half_ref, wide_ref):
    for m in range(NMASS):
        wide_ref[pl.ds(PER * m, PER), :] = load_ref[m % 2, m // 2].astype(F32)
    half_ref[...] = wide_ref[...].astype(BF16)
    for y in range(NY):
        out_ref[y, pl.ds(0, TOPS), :] = jnp.zeros((TOPS, TILE), F32)
    count = meta_ref[CAP]
    for s in range(CAP):
        place = meta_ref[s]
        row, col = place // TCOLS, place % TCOLS
        lanes = pl.ds(pl.multiple_of(row * TILE, TILE), TILE)
        product = jnp.dot(half_ref[:, lanes], tiles_ref[s], preferred_element_type=F32) * TOP_SCALE
        rows = pl.ds(pl.multiple_of((col // NY) * RANK, RANK), RANK)
        out_ref[col % NY, rows, :] += jnp.where(s < count, product, 0.0)
    half = half_ref[...]
    gram = lax.dot_general(half, half, CONTRACT_LAST, preferred_element_type=F32) * GRAM_SCALE
    packed = jnp.concatenate([gram[16 * i : 16 * i + 16, :] for i in range(4)], axis=1)
    for y in range(NY):
        for z in range(NZ):
            c = z * NY + y
            out_ref[y, pl.ds(TOPS + 2 * z, 2), :] = sent_ref[:, pl.ds(c * TILE, TILE)]
        out_ref[y, pl.ds(TOPS + 2 * NZ, 16), :] = packed


def update_kernel(sums_ref, spec_ref, out_ref):
    packed = sums_ref[pl.ds(RANK, 16), :] * (TOP_SCALE / GRAM_SCALE)
    gram = jnp.concatenate([packed[:, RANK * i : RANK * i + RANK] for i in range(4)], axis=0)
    spec = spec_ref[...]
    bottom = jnp.dot(gram, spec.astype(BF16).astype(F32), precision=lax.Precision.HIGHEST, preferred_element_type=F32)
    new = spec * sums_ref[pl.ds(0, RANK), :] / bottom
    fresh = new.astype(BF16)
    rest = new - fresh.astype(F32)
    for z in range(NZ):
        out_ref[z, pl.ds(0, RANK), :] = fresh
        out_ref[z, pl.ds(RANK, 8), :] = rest[8 * z : 8 * z + 8, :].astype(BF16)


def spread_kernel(in_ref, out_ref):
    for y in range(NY):
        for z in range(NZ):
            out_ref[y, pl.ds(z * RANK, RANK), :] = in_ref[z, pl.ds(0, RANK), :]
    for z in range(NZ):
        rest = in_ref[z, pl.ds(RANK, 8), :].astype(F32)
        for y in range(NY):
            out_ref[y, pl.ds(TOPS + 2 * z, 2), :] = rest[2 * y : 2 * y + 2, :].astype(BF16)


def load_kernel(meta_ref, fresh_ref, tiles_ref, out_ref, acc_ref):
    acc_ref[...] = jnp.zeros_like(acc_ref)
    count = meta_ref[CAP]
    for s in range(CAP):
        place = meta_ref[s]
        row, col = place // TCOLS, place % TCOLS
        rows = pl.ds(pl.multiple_of((col // NY) * RANK, RANK), RANK)
        block = fresh_ref[col % NY, rows, :]
        product = lax.dot_general(block, tiles_ref[s], CONTRACT_LAST, preferred_element_type=F32)
        lanes = pl.ds(pl.multiple_of(row * TILE, TILE), TILE)
        acc_ref[:, lanes] += jnp.where(s < count, product, 0.0)
    gram = jnp.zeros((RANK, RANK), F32)
    for y in range(NY):
        for z in range(NZ):
            block = fresh_ref[y, pl.ds(z * RANK, RANK), :]
            gram = gram + lax.dot_general(block, block, CONTRACT_LAST, preferred_element_type=F32)
    top = acc_ref[...]
    tail = jnp.concatenate([gram, jnp.zeros((RANK, RANK), F32)], axis=1)
    for m in range(NMASS):
        rows = pl.ds(PER * (m // 2), PER)
        out_ref[m % 2, rows, pl.ds(0, PIXELS)] = top[PER * m : PER * m + PER, :]
        out_ref[m % 2, rows, pl.ds(PIXELS, 128)] = tail[PER * m : PER * m + PER, :]


def encode_kernel(in_ref, out_ref):
    total = in_ref[0] + in_ref[1]

    def exponent(x):
        return jnp.floor(jnp.log2(jnp.maximum(jnp.max(x, axis=1, keepdims=True), 1e-30))) - 13.0

    top, gram = total[:, :PIXELS], total[:, PIXELS : PIXELS + RANK]
    top_exp, gram_exp = exponent(top), exponent(gram)
    top = top * jnp.exp2(-top_exp)
    gram = gram * jnp.exp2(-gram_exp)
    lane = lax.broadcasted_iota(jnp.int32, gram.shape, 1)
    tail = jnp.where(lane == 0, top_exp, jnp.where(lane == 1, gram_exp, 0.0))
    tail = jnp.concatenate([gram, tail], axis=1)
    for m in range(NMASS // 2):
        out_ref[m, :, pl.ds(0, PIXELS)] = top[PER * m : PER * m + PER, :]
        out_ref[m, :, pl.ds(PIXELS, 128)] = tail[PER * m : PER * m + PER, :]


def final_kernel(part_ref, half_ref, loading_ref, out_ref):
    top = jnp.zeros((PER, PIXELS), F32)
    gram = jnp.zeros((PER, RANK), F32)
    for m in range(NMASS // 2):
        tail = part_ref[m, :, pl.ds(PIXELS, 128)]
        top = top + part_ref[m, :, pl.ds(0, PIXELS)] * jnp.exp2(tail[:, RANK : RANK + 1])
        gram = gram + tail[:, :RANK] * jnp.exp2(tail[:, RANK + 1 : RANK + 2])
    bottom = jnp.dot(gram, half_ref[...].astype(F32), precision=lax.Precision.HIGHEST, preferred_element_type=F32)
    out_ref[...] = loading_ref[...] * top / bottom


def spectra_kernel(place_ref, recv_ref, spec_ref, out_ref):
    zl, yl = place_ref[0], place_ref[1]
    for z in range(NZ):
        for y in range(NY):
            c = z * NY + y
            eight = recv_ref[y, pl.ds(pl.multiple_of(z * RANK + 8 * zl, 8), 8), :].astype(F32)
            two = eight[0:2, :]
            for k in range(1, NY):
                two = jnp.where(yl == k, eight[2 * k : 2 * k + 2, :], two)
            rest = recv_ref[y, pl.ds(TOPS + 2 * z, 2), :].astype(F32)
            cols = pl.ds(c * TILE, TILE)
            spec = spec_ref[:, cols]
            out_ref[:, cols] = (two + rest) * (spec / half_precision(spec))


def near(x):
    return pltpu.with_memory_space_constraint(x, pltpu.VMEM)


def call(body, out, *operands, scratch=(), pinned=True):
    specs = [SMEM if x.dtype == jnp.int32 else VMEM for x in operands]
    return pl.pallas_call(
        body,
        out_shape=out,
        in_specs=specs,
        out_specs=jax.tree.map(lambda _: VMEM, out),
        scratch_shapes=scratch,
        compiler_params=PARAMS,
        name=body.__name__,
    )(*[near(x) if pinned and x.dtype != jnp.int32 else x for x in operands])


def local(tiles, tile_pos, kept_tile_count, loading, spectra):
    tiles = tiles[0, 0]
    meta = jnp.concatenate([tile_pos[0, 0], kept_tile_count[0]])

    load = call(own_kernel, pltpu.VMEM((NMASS // 2, PER, PIXELS), BF16), loading, pinned=False)
    load = lax.all_to_all(load, ("zh", "x"), 0, 0, tiled=True)
    load = lax.all_gather(load, "core", axis=0, tiled=False)
    tiles, sent = pl.pallas_call(
        fetch_kernel,
        out_shape=(pltpu.VMEM(tiles.shape, BF16), pltpu.VMEM(spectra.shape, F32)),
        in_specs=[pl.BlockSpec(memory_space=pl.ANY), VMEM],
        out_specs=(VMEM, VMEM),
        scratch_shapes=[pltpu.SemaphoreType.DMA],
        compiler_params=PARAMS,
        name="fetch_kernel",
    )(tiles, spectra)

    out, half = call(
        spec_kernel,
        (pltpu.VMEM((NY, TOPS + 32, TILE), F32), pltpu.VMEM((RANK, PIXELS), BF16)),
        meta, load, tiles, sent,
        scratch=[pltpu.VMEM((RANK, PIXELS), F32)],
    )
    part = lax.all_to_all(out.astype(F16), "y", 0, 0, tiled=True)
    tops = part[:, :TOPS].astype(F32).sum(0).astype(F16).reshape(NZ, RANK, TILE)
    old = part[:, TOPS : TOPS + 2 * NZ].reshape(NY, NZ, 2, TILE).transpose(1, 0, 2, 3).reshape(NZ, 8, TILE)
    gram = part[:, TOPS + 2 * NZ :].astype(F32).sum(0).astype(F16)
    gram = jnp.broadcast_to(gram[None], (NZ, 16, TILE))
    part = lax.all_to_all(jnp.concatenate([tops, old, gram], axis=1), "zl", 0, 0, tiled=True)
    wide = part.astype(F32)
    sums = jnp.concatenate([wide[:, :RANK].sum(0), wide[:, RANK + 8 :].sum(0)], axis=0)
    old = wide[:, RANK : RANK + 8].reshape(RANK, TILE)

    fresh = call(update_kernel, pltpu.VMEM((NZ, RANK + 8, TILE), BF16), sums, old)
    fresh = lax.all_to_all(fresh, "zl", 0, 0, tiled=True)
    fresh = call(spread_kernel, pltpu.VMEM((NY, TOPS + 16, TILE), BF16), fresh)
    fresh = lax.all_to_all(fresh, "y", 0, 0, tiled=True)

    out = call(
        load_kernel,
        pltpu.VMEM((2, RANK // 2, WIDE), F32),
        meta, fresh, tiles,
        scratch=[pltpu.VMEM((RANK, PIXELS), F32)],
    )
    part = lax.all_to_all(out, "core", 0, 0, tiled=True)
    part = call(encode_kernel, pltpu.VMEM((NMASS // 2, PER, WIDE), F32), part)
    part = lax.all_to_all(part.astype(F16), ("zh", "x"), 0, 0, tiled=True).astype(F32)

    place = jnp.stack([lax.axis_index("zl"), lax.axis_index("y")]).astype(jnp.int32)
    spectra_new = call(spectra_kernel, jax.ShapeDtypeStruct(spectra.shape, F32), place, fresh, spectra)
    loading_new = call(final_kernel, jax.ShapeDtypeStruct(loading.shape, F32), part, half, loading)
    return (loading_new, spectra_new)


def solution(mesh):
    fine = Mesh(mesh.devices.reshape(NZ, NY, 2, 4, 2), PIX + MASS)
    return jax.shard_map(
        local,
        mesh=fine,
        in_specs=(P(PIX, MASS, None, None, None), P(PIX, MASS, None), P(PIX, MASS), P(MASS, PIX), P(PIX, MASS)),
        out_specs=(P(MASS, PIX), P(PIX, MASS)),
        check_vma=False,
    )
```

```python
import jax
import jax.numpy as jnp
from jax import lax
from jax.experimental import pallas as pl
from jax.experimental.pallas import tpu as pltpu
from jax.sharding import Mesh, PartitionSpec as P

F32, BF16, F16 = jnp.float32, jnp.bfloat16, jnp.float16
PIX = ("p", "q")
MASS = ("zh", "x", "core")
RANK, TILE, TROWS, TCOLS, CAP = 64, 256, 8, 32, 16
NZ, NY, NMASS = 4, 8, 16
OWN = RANK // NZ
PER = RANK // NMASS
TOP_SCALE = 2.0**-10
GRAM_SCALE = 2.0**-3
TOPS = NZ * RANK
PIXELS = TROWS * TILE
WIDE = PIXELS + 128
VMEM = pl.BlockSpec(memory_space=pltpu.VMEM)
SMEM = pl.BlockSpec(memory_space=pltpu.SMEM)
PARAMS = pltpu.CompilerParams(vmem_limit_bytes=12 << 20)
CONTRACT_LAST = (((1,), (1,)), ((), ()))


def half_precision(x):
    wide = x * 8193.0
    return wide - (wide - x)


def own_kernel(loading_ref, out_ref):
    half = loading_ref[...].astype(BF16)
    for m in range(NMASS // 2):
        out_ref[m] = half


def fetch_kernel(tiles_ref, spec_ref, out_ref, sent_ref, sem):
    copy = pltpu.make_async_copy(tiles_ref, out_ref, sem)
    copy.start()
    sent_ref[...] = half_precision(spec_ref[...])
    copy.wait()


def spec_kernel(meta_ref, load_ref, tiles_ref, sent_ref, out_ref, half_ref, wide_ref):
    for m in range(NMASS):
        wide_ref[pl.ds(PER * m, PER), :] = load_ref[m % 2, m // 2].astype(F32)
    half_ref[...] = wide_ref[...].astype(BF16)
    for y in range(NY):
        out_ref[y, pl.ds(0, TOPS), :] = jnp.zeros((TOPS, TILE), F32)
    count = meta_ref[CAP]
    for s in range(CAP):
        place = meta_ref[s]
        row, col = place // TCOLS, place % TCOLS
        lanes = pl.ds(pl.multiple_of(row * TILE, TILE), TILE)
        product = jnp.dot(half_ref[:, lanes], tiles_ref[s], preferred_element_type=F32) * TOP_SCALE
        rows = pl.ds(pl.multiple_of((col // NY) * RANK, RANK), RANK)
        out_ref[col % NY, rows, :] += jnp.where(s < count, product, 0.0)
    half = half_ref[...]
    gram = lax.dot_general(half, half, CONTRACT_LAST, preferred_element_type=F32) * GRAM_SCALE
    packed = jnp.concatenate([gram[16 * i : 16 * i + 16, :] for i in range(4)], axis=1)
    for y in range(NY):
        for z in range(NZ):
            c = z * NY + y
            out_ref[y, pl.ds(TOPS + 2 * z, 2), :] = sent_ref[:, pl.ds(c * TILE, TILE)]
        out_ref[y, pl.ds(TOPS + 2 * NZ, 16), :] = packed


def middle_kernel(in_ref, out_ref):
    gram = in_ref[0, pl.ds(TOPS + 2 * NZ, 16), :]
    for y in range(1, NY):
        gram = gram + in_ref[y, pl.ds(TOPS + 2 * NZ, 16), :]
    for z in range(NZ):
        rows = pl.ds(z * RANK, RANK)
        top = in_ref[0, rows, :]
        for y in range(1, NY):
            top = top + in_ref[y, rows, :]
        out_ref[z, pl.ds(0, RANK), :] = top
        for y in range(NY):
            out_ref[z, pl.ds(RANK + 2 * y, 2), :] = in_ref[y, pl.ds(TOPS + 2 * z, 2), :]
        out_ref[z, pl.ds(RANK + OWN, 16), :] = gram


def update_kernel(in_ref, out_ref):
    packed = in_ref[0, pl.ds(RANK + OWN, 16), :]
    top = in_ref[0, pl.ds(0, RANK), :]
    for z in range(1, NZ):
        packed = packed + in_ref[z, pl.ds(RANK + OWN, 16), :]
        top = top + in_ref[z, pl.ds(0, RANK), :]
    packed = packed * (TOP_SCALE / GRAM_SCALE)
    gram = jnp.concatenate([packed[:, RANK * i : RANK * i + RANK] for i in range(4)], axis=0)
    spec = jnp.concatenate([in_ref[z, pl.ds(RANK, OWN), :] for z in range(NZ)], axis=0)
    bottom = jnp.dot(gram, spec.astype(BF16).astype(F32), precision=lax.Precision.HIGHEST, preferred_element_type=F32)
    new = spec * top / bottom
    fresh = new.astype(BF16)
    rest = new - fresh.astype(F32)
    for z in range(NZ):
        out_ref[z, pl.ds(0, RANK), :] = fresh
        out_ref[z, pl.ds(RANK, OWN), :] = rest[OWN * z : OWN * z + OWN, :].astype(BF16)


def spread_kernel(in_ref, out_ref):
    for y in range(NY):
        for z in range(NZ):
            out_ref[y, pl.ds(z * RANK, RANK), :] = in_ref[z, pl.ds(0, RANK), :]
    for z in range(NZ):
        rest = in_ref[z, pl.ds(RANK, OWN), :].astype(F32)
        for y in range(NY):
            out_ref[y, pl.ds(TOPS + 2 * z, 2), :] = rest[2 * y : 2 * y + 2, :].astype(BF16)


def load_kernel(meta_ref, fresh_ref, tiles_ref, out_ref, acc_ref):
    acc_ref[...] = jnp.zeros_like(acc_ref)
    count = meta_ref[CAP]
    for s in range(CAP):
        place = meta_ref[s]
        row, col = place // TCOLS, place % TCOLS
        rows = pl.ds(pl.multiple_of((col // NY) * RANK, RANK), RANK)
        block = fresh_ref[col % NY, rows, :]
        product = lax.dot_general(block, tiles_ref[s], CONTRACT_LAST, preferred_element_type=F32)
        lanes = pl.ds(pl.multiple_of(row * TILE, TILE), TILE)
        acc_ref[:, lanes] += jnp.where(s < count, product, 0.0)
    gram = jnp.zeros((RANK, RANK), F32)
    for y in range(NY):
        for z in range(NZ):
            block = fresh_ref[y, pl.ds(z * RANK, RANK), :]
            gram = gram + lax.dot_general(block, block, CONTRACT_LAST, preferred_element_type=F32)
    top = acc_ref[...]
    tail = jnp.concatenate([gram, jnp.zeros((RANK, RANK), F32)], axis=1)
    for m in range(NMASS):
        rows = pl.ds(PER * (m // 2), PER)
        out_ref[m % 2, rows, pl.ds(0, PIXELS)] = top[PER * m : PER * m + PER, :]
        out_ref[m % 2, rows, pl.ds(PIXELS, 128)] = tail[PER * m : PER * m + PER, :]


def encode_kernel(in_ref, out_ref):
    total = in_ref[0] + in_ref[1]

    def exponent(x):
        return jnp.floor(jnp.log2(jnp.maximum(jnp.max(x, axis=1, keepdims=True), 1e-30))) - 13.0

    top, gram = total[:, :PIXELS], total[:, PIXELS : PIXELS + RANK]
    top_exp, gram_exp = exponent(top), exponent(gram)
    top = top * jnp.exp2(-top_exp)
    gram = gram * jnp.exp2(-gram_exp)
    lane = lax.broadcasted_iota(jnp.int32, gram.shape, 1)
    tail = jnp.where(lane == 0, top_exp, jnp.where(lane == 1, gram_exp, 0.0))
    tail = jnp.concatenate([gram, tail], axis=1)
    for m in range(NMASS // 2):
        out_ref[m, :, pl.ds(0, PIXELS)] = top[PER * m : PER * m + PER, :]
        out_ref[m, :, pl.ds(PIXELS, 128)] = tail[PER * m : PER * m + PER, :]


def final_kernel(part_ref, half_ref, loading_ref, out_ref):
    top = jnp.zeros((PER, PIXELS), F32)
    gram = jnp.zeros((PER, RANK), F32)
    for m in range(NMASS // 2):
        tail = part_ref[m, :, pl.ds(PIXELS, 128)]
        top = top + part_ref[m, :, pl.ds(0, PIXELS)] * jnp.exp2(tail[:, RANK : RANK + 1])
        gram = gram + tail[:, :RANK] * jnp.exp2(tail[:, RANK + 1 : RANK + 2])
    bottom = jnp.dot(gram, half_ref[...].astype(F32), precision=lax.Precision.HIGHEST, preferred_element_type=F32)
    out_ref[...] = loading_ref[...] * top / bottom


def spectra_kernel(place_ref, recv_ref, spec_ref, out_ref):
    zl, yl = place_ref[0], place_ref[1]
    for z in range(NZ):
        for y in range(NY):
            c = z * NY + y
            own = recv_ref[y, pl.ds(pl.multiple_of(z * RANK + OWN * zl, OWN), OWN), :].astype(F32)
            two = own[0:2, :]
            for k in range(1, NY):
                two = jnp.where(yl == k, own[2 * k : 2 * k + 2, :], two)
            rest = recv_ref[y, pl.ds(TOPS + 2 * z, 2), :].astype(F32)
            cols = pl.ds(c * TILE, TILE)
            spec = spec_ref[:, cols]
            out_ref[:, cols] = (two + rest) * (spec / half_precision(spec))


def near(x):
    return pltpu.with_memory_space_constraint(x, pltpu.VMEM)


def call(body, out, *operands, scratch=(), pinned=True):
    specs = [SMEM if x.dtype == jnp.int32 else VMEM for x in operands]
    return pl.pallas_call(
        body,
        out_shape=out,
        in_specs=specs,
        out_specs=jax.tree.map(lambda _: VMEM, out),
        scratch_shapes=scratch,
        compiler_params=PARAMS,
        name=body.__name__,
    )(*[near(x) if pinned and x.dtype != jnp.int32 else x for x in operands])


def local(tiles, tile_pos, kept_tile_count, loading, spectra):
    tiles = tiles[0, 0]
    meta = jnp.concatenate([tile_pos[0, 0], kept_tile_count[0]])

    load = call(own_kernel, pltpu.VMEM((NMASS // 2, PER, PIXELS), BF16), loading, pinned=False)
    load = lax.all_to_all(load, ("zh", "x"), 0, 0, tiled=True)
    load = lax.all_gather(load, "core", axis=0, tiled=False)
    tiles, sent = pl.pallas_call(
        fetch_kernel,
        out_shape=(pltpu.VMEM(tiles.shape, BF16), pltpu.VMEM(spectra.shape, F32)),
        in_specs=[pl.BlockSpec(memory_space=pl.ANY), VMEM],
        out_specs=(VMEM, VMEM),
        scratch_shapes=[pltpu.SemaphoreType.DMA],
        compiler_params=PARAMS,
        name="fetch_kernel",
    )(tiles, spectra)

    out, half = call(
        spec_kernel,
        (pltpu.VMEM((NY, TOPS + 2 * NZ + 16, TILE), F32), pltpu.VMEM((RANK, PIXELS), BF16)),
        meta, load, tiles, sent,
        scratch=[pltpu.VMEM((RANK, PIXELS), F32)],
    )
    part = lax.all_to_all(out.astype(F16), "q", 0, 0, tiled=True)
    part = call(middle_kernel, pltpu.VMEM((NZ, RANK + OWN + 16, TILE), F32), part.astype(F32))
    part = lax.all_to_all(part.astype(F16), "p", 0, 0, tiled=True)

    fresh = call(update_kernel, pltpu.VMEM((NZ, RANK + OWN, TILE), BF16), part.astype(F32))
    fresh = lax.all_to_all(fresh, "p", 0, 0, tiled=True)
    fresh = call(spread_kernel, pltpu.VMEM((NY, TOPS + 2 * NZ, TILE), BF16), fresh)
    fresh = lax.all_to_all(fresh, "q", 0, 0, tiled=True)

    out = call(
        load_kernel,
        pltpu.VMEM((2, RANK // 2, WIDE), F32),
        meta, fresh, tiles,
        scratch=[pltpu.VMEM((RANK, PIXELS), F32)],
    )
    part = lax.all_to_all(out, "core", 0, 0, tiled=True)
    part = call(encode_kernel, pltpu.VMEM((NMASS // 2, PER, WIDE), F32), part)
    part = lax.all_to_all(part.astype(F16), ("zh", "x"), 0, 0, tiled=True).astype(F32)

    place = jnp.stack([lax.axis_index("p"), lax.axis_index("q")]).astype(jnp.int32)
    spectra_new = call(spectra_kernel, jax.ShapeDtypeStruct(spectra.shape, F32), place, fresh, spectra)
    loading_new = call(final_kernel, jax.ShapeDtypeStruct(loading.shape, F32), part, half, loading)
    return (loading_new, spectra_new)


def solution(mesh):
    fine = Mesh(mesh.devices.reshape(NZ, NY, 2, 4, 2), PIX + MASS)
    return jax.shard_map(
        local,
        mesh=fine,
        in_specs=(P(PIX, MASS, None, None, None), P(PIX, MASS, None), P(PIX, MASS), P(MASS, PIX), P(PIX, MASS)),
        out_specs=(P(MASS, PIX), P(PIX, MASS)),
        check_vma=False,
    )
```

```python
import jax
import jax.numpy as jnp
from jax import lax
from jax.experimental import pallas as pl
from jax.experimental.pallas import tpu as pltpu
from jax.sharding import Mesh, PartitionSpec as P

F32, BF16, F16 = jnp.float32, jnp.bfloat16, jnp.float16
PIX = ("p", "q")
MASS = ("zh", "x", "core")
RANK, TILE, TROWS, TCOLS, CAP = 64, 256, 8, 32, 16
NZ, NY, NMASS = 4, 8, 16
OWN = RANK // NZ
PER = RANK // NMASS
TOP_SCALE = 2.0**-11
GRAM_SCALE = 2.0**-4
TOPS = NZ * RANK
PIXELS = TROWS * TILE
WIDE = PIXELS + 128
VMEM = pl.BlockSpec(memory_space=pltpu.VMEM)
SMEM = pl.BlockSpec(memory_space=pltpu.SMEM)
PARAMS = pltpu.CompilerParams(vmem_limit_bytes=12 << 20)
CONTRACT_LAST = (((1,), (1,)), ((), ()))


def half_precision(x):
    wide = x * 8193.0
    return wide - (wide - x)


def own_kernel(loading_ref, out_ref):
    half = loading_ref[...].astype(BF16)
    for m in range(NMASS // 2):
        out_ref[m] = half


def fetch_kernel(tiles_ref, spec_ref, out_ref, sent_ref, sem):
    copy = pltpu.make_async_copy(tiles_ref, out_ref, sem)
    copy.start()
    sent_ref[...] = half_precision(spec_ref[...])
    copy.wait()


def spec_kernel(meta_ref, load_ref, tiles_ref, sent_ref, out_ref, half_ref, wide_ref):
    for m in range(NMASS):
        wide_ref[pl.ds(PER * m, PER), :] = load_ref[m % 2, m // 2].astype(F32)
    half_ref[...] = wide_ref[...].astype(BF16)
    for y in range(NY):
        out_ref[y, pl.ds(0, TOPS), :] = jnp.zeros((TOPS, TILE), F32)
    count = meta_ref[CAP]
    for s in range(CAP):
        place = meta_ref[s]
        row, col = place // TCOLS, place % TCOLS
        lanes = pl.ds(pl.multiple_of(row * TILE, TILE), TILE)
        product = jnp.dot(half_ref[:, lanes], tiles_ref[s], preferred_element_type=F32) * TOP_SCALE
        rows = pl.ds(pl.multiple_of((col // NY) * RANK, RANK), RANK)
        out_ref[col % NY, rows, :] += jnp.where(s < count, product, 0.0)
    half = half_ref[...]
    gram = lax.dot_general(half, half, CONTRACT_LAST, preferred_element_type=F32) * GRAM_SCALE
    packed = jnp.concatenate([gram[16 * i : 16 * i + 16, :] for i in range(4)], axis=1)
    for y in range(NY):
        for z in range(NZ):
            c = z * NY + y
            out_ref[y, pl.ds(TOPS + 2 * z, 2), :] = sent_ref[:, pl.ds(c * TILE, TILE)]
        out_ref[y, pl.ds(TOPS + 2 * NZ, 16), :] = packed


def middle_kernel(in_ref, out_ref):
    gram = in_ref[0, pl.ds(TOPS + 2 * NZ, 16), :]
    for y in range(1, NY):
        gram = gram + in_ref[y, pl.ds(TOPS + 2 * NZ, 16), :]
    for z in range(NZ):
        rows = pl.ds(z * RANK, RANK)
        top = in_ref[0, rows, :]
        for y in range(1, NY):
            top = top + in_ref[y, rows, :]
        out_ref[z, pl.ds(0, RANK), :] = top
        for y in range(NY):
            out_ref[z, pl.ds(RANK + 2 * y, 2), :] = in_ref[y, pl.ds(TOPS + 2 * z, 2), :]
        out_ref[z, pl.ds(RANK + OWN, 16), :] = gram


def update_kernel(in_ref, out_ref):
    packed = in_ref[0, pl.ds(RANK + OWN, 16), :]
    top = in_ref[0, pl.ds(0, RANK), :]
    for z in range(1, NZ):
        packed = packed + in_ref[z, pl.ds(RANK + OWN, 16), :]
        top = top + in_ref[z, pl.ds(0, RANK), :]
    packed = packed * (TOP_SCALE / GRAM_SCALE)
    gram = jnp.concatenate([packed[:, RANK * i : RANK * i + RANK] for i in range(4)], axis=0)
    spec = jnp.concatenate([in_ref[z, pl.ds(RANK, OWN), :] for z in range(NZ)], axis=0)
    bottom = jnp.dot(gram, spec.astype(BF16).astype(F32), precision=lax.Precision.HIGHEST, preferred_element_type=F32)
    new = spec * top / bottom
    fresh = new.astype(BF16)
    rest = new - fresh.astype(F32)
    for z in range(NZ):
        out_ref[z, pl.ds(0, RANK), :] = fresh
        out_ref[z, pl.ds(RANK, OWN), :] = rest[OWN * z : OWN * z + OWN, :].astype(BF16)


def spread_kernel(in_ref, out_ref):
    for y in range(NY):
        for z in range(NZ):
            out_ref[y, pl.ds(z * RANK, RANK), :] = in_ref[z, pl.ds(0, RANK), :]
    for z in range(NZ):
        rest = in_ref[z, pl.ds(RANK, OWN), :].astype(F32)
        for y in range(NY):
            out_ref[y, pl.ds(TOPS + 2 * z, 2), :] = rest[2 * y : 2 * y + 2, :].astype(BF16)


def load_kernel(meta_ref, fresh_ref, tiles_ref, out_ref, acc_ref):
    acc_ref[...] = jnp.zeros_like(acc_ref)
    count = meta_ref[CAP]
    for s in range(CAP):
        place = meta_ref[s]
        row, col = place // TCOLS, place % TCOLS
        rows = pl.ds(pl.multiple_of((col // NY) * RANK, RANK), RANK)
        block = fresh_ref[col % NY, rows, :]
        product = lax.dot_general(block, tiles_ref[s], CONTRACT_LAST, preferred_element_type=F32)
        lanes = pl.ds(pl.multiple_of(row * TILE, TILE), TILE)
        acc_ref[:, lanes] += jnp.where(s < count, product, 0.0)
    gram = jnp.zeros((RANK, RANK), F32)
    for y in range(NY):
        for z in range(NZ):
            block = fresh_ref[y, pl.ds(z * RANK, RANK), :]
            gram = gram + lax.dot_general(block, block, CONTRACT_LAST, preferred_element_type=F32)
    top = acc_ref[...]
    tail = jnp.concatenate([gram, jnp.zeros((RANK, RANK), F32)], axis=1)
    for m in range(NMASS):
        rows = pl.ds(PER * (m // 2), PER)
        out_ref[m % 2, rows, pl.ds(0, PIXELS)] = top[PER * m : PER * m + PER, :]
        out_ref[m % 2, rows, pl.ds(PIXELS, 128)] = tail[PER * m : PER * m + PER, :]


def encode_kernel(in_ref, out_ref):
    total = in_ref[0] + in_ref[1]

    def exponent(x):
        return jnp.floor(jnp.log2(jnp.maximum(jnp.max(x, axis=1, keepdims=True), 1e-30))) - 13.0

    top, gram = total[:, :PIXELS], total[:, PIXELS : PIXELS + RANK]
    top_exp, gram_exp = exponent(top), exponent(gram)
    top = top * jnp.exp2(-top_exp)
    gram = gram * jnp.exp2(-gram_exp)
    lane = lax.broadcasted_iota(jnp.int32, gram.shape, 1)
    tail = jnp.where(lane == 0, top_exp, jnp.where(lane == 1, gram_exp, 0.0))
    tail = jnp.concatenate([gram, tail], axis=1)
    for m in range(NMASS // 2):
        out_ref[m, :, pl.ds(0, PIXELS)] = top[PER * m : PER * m + PER, :]
        out_ref[m, :, pl.ds(PIXELS, 128)] = tail[PER * m : PER * m + PER, :]


def final_kernel(part_ref, half_ref, loading_ref, out_ref):
    top = jnp.zeros((PER, PIXELS), F32)
    gram = jnp.zeros((PER, RANK), F32)
    for m in range(NMASS // 2):
        tail = part_ref[m, :, pl.ds(PIXELS, 128)]
        top = top + part_ref[m, :, pl.ds(0, PIXELS)] * jnp.exp2(tail[:, RANK : RANK + 1])
        gram = gram + tail[:, :RANK] * jnp.exp2(tail[:, RANK + 1 : RANK + 2])
    bottom = jnp.dot(gram, half_ref[...].astype(F32), precision=lax.Precision.HIGHEST, preferred_element_type=F32)
    out_ref[...] = loading_ref[...] * top / bottom


def spectra_kernel(place_ref, recv_ref, spec_ref, out_ref):
    zl, yl = place_ref[0], place_ref[1]
    for z in range(NZ):
        for y in range(NY):
            c = z * NY + y
            own = recv_ref[y, pl.ds(pl.multiple_of(z * RANK + OWN * zl, OWN), OWN), :].astype(F32)
            two = own[0:2, :]
            for k in range(1, NY):
                two = jnp.where(yl == k, own[2 * k : 2 * k + 2, :], two)
            rest = recv_ref[y, pl.ds(TOPS + 2 * z, 2), :].astype(F32)
            cols = pl.ds(c * TILE, TILE)
            spec = spec_ref[:, cols]
            out_ref[:, cols] = (two + rest) * (spec / half_precision(spec))


def near(x):
    return pltpu.with_memory_space_constraint(x, pltpu.VMEM)


def call(body, out, *operands, scratch=(), pinned=True):
    specs = [SMEM if x.dtype == jnp.int32 else VMEM for x in operands]
    return pl.pallas_call(
        body,
        out_shape=out,
        in_specs=specs,
        out_specs=jax.tree.map(lambda _: VMEM, out),
        scratch_shapes=scratch,
        compiler_params=PARAMS,
        name=body.__name__,
    )(*[near(x) if pinned and x.dtype != jnp.int32 else x for x in operands])


def local(tiles, tile_pos, kept_tile_count, loading, spectra):
    tiles = tiles[0, 0]
    meta = jnp.concatenate([tile_pos[0, 0], kept_tile_count[0]])

    load = call(own_kernel, pltpu.VMEM((NMASS // 2, PER, PIXELS), BF16), loading, pinned=False)
    load = lax.all_to_all(load, ("zh", "x"), 0, 0, tiled=True)
    load = lax.all_gather(load, "core", axis=0, tiled=False)
    tiles, sent = pl.pallas_call(
        fetch_kernel,
        out_shape=(pltpu.VMEM(tiles.shape, BF16), pltpu.VMEM(spectra.shape, F32)),
        in_specs=[pl.BlockSpec(memory_space=pl.ANY), VMEM],
        out_specs=(VMEM, VMEM),
        scratch_shapes=[pltpu.SemaphoreType.DMA],
        compiler_params=PARAMS,
        name="fetch_kernel",
    )(tiles, spectra)

    out, half = call(
        spec_kernel,
        (pltpu.VMEM((NY, TOPS + 2 * NZ + 16, TILE), F32), pltpu.VMEM((RANK, PIXELS), BF16)),
        meta, load, tiles, sent,
        scratch=[pltpu.VMEM((RANK, PIXELS), F32)],
    )
    part = lax.all_to_all(out.astype(F16), "q", 0, 0, tiled=True)
    part = call(middle_kernel, pltpu.VMEM((NZ, RANK + OWN + 16, TILE), F32), part.astype(F32))
    part = lax.all_to_all(part.astype(F16), "p", 0, 0, tiled=True)

    fresh = call(update_kernel, pltpu.VMEM((NZ, RANK + OWN, TILE), BF16), part.astype(F32))
    fresh = lax.all_to_all(fresh, "p", 0, 0, tiled=True)
    fresh = call(spread_kernel, pltpu.VMEM((NY, TOPS + 2 * NZ, TILE), BF16), fresh)
    fresh = lax.all_to_all(fresh, "q", 0, 0, tiled=True)

    out = call(
        load_kernel,
        pltpu.VMEM((2, RANK // 2, WIDE), F32),
        meta, fresh, tiles,
        scratch=[pltpu.VMEM((RANK, PIXELS), F32)],
    )
    part = lax.all_to_all(out, "core", 0, 0, tiled=True)
    part = call(encode_kernel, pltpu.VMEM((NMASS // 2, PER, WIDE), F32), part)
    part = lax.all_to_all(part.astype(F16), ("zh", "x"), 0, 0, tiled=True).astype(F32)

    place = jnp.stack([lax.axis_index("p"), lax.axis_index("q")]).astype(jnp.int32)
    spectra_new = call(spectra_kernel, jax.ShapeDtypeStruct(spectra.shape, F32), place, fresh, spectra)
    loading_new = call(final_kernel, jax.ShapeDtypeStruct(loading.shape, F32), part, half, loading)
    return (loading_new, spectra_new)


def solution(mesh):
    fine = Mesh(mesh.devices.reshape(NZ, NY, 2, 4, 2), PIX + MASS)
    return jax.shard_map(
        local,
        mesh=fine,
        in_specs=(P(PIX, MASS, None, None, None), P(PIX, MASS, None), P(PIX, MASS), P(MASS, PIX), P(PIX, MASS)),
        out_specs=(P(MASS, PIX), P(PIX, MASS)),
        check_vma=False,
    )
```

```python
import jax
import jax.numpy as jnp
from jax import lax
from jax.experimental import pallas as pl
from jax.experimental.pallas import tpu as pltpu
from jax.sharding import Mesh, PartitionSpec as P

F32, BF16, F16 = jnp.float32, jnp.bfloat16, jnp.float16
PIX = ("p", "q")
MASS = ("zh", "x", "core")
RANK, TILE, TROWS, TCOLS, CAP = 64, 256, 8, 32, 16
NZ, NY, NMASS = 4, 8, 16
OWN = RANK // NZ
PER = RANK // NMASS
TOP_SCALE = 2.0**-11
GRAM_SCALE = 2.0**-4
TOPS = NZ * RANK
PIXELS = TROWS * TILE
WIDE = PIXELS + 128
VMEM = pl.BlockSpec(memory_space=pltpu.VMEM)
SMEM = pl.BlockSpec(memory_space=pltpu.SMEM)
PARAMS = pltpu.CompilerParams(vmem_limit_bytes=12 << 20)
CONTRACT_LAST = (((1,), (1,)), ((), ()))


def half_precision(x):
    wide = x * 8193.0
    return wide - (wide - x)


def own_kernel(loading_ref, out_ref):
    half = loading_ref[...].astype(BF16)
    for m in range(NMASS // 2):
        out_ref[m] = half


def fetch_kernel(tiles_ref, spec_ref, out_ref, sent_ref, sem):
    copy = pltpu.make_async_copy(tiles_ref, out_ref, sem)
    copy.start()
    sent_ref[...] = half_precision(spec_ref[...])
    copy.wait()


def spec_kernel(meta_ref, load_ref, tiles_ref, sent_ref, out_ref, half_ref, wide_ref):
    for m in range(NMASS):
        wide_ref[pl.ds(PER * m, PER), :] = load_ref[m % 2, m // 2].astype(F32)
    half_ref[...] = wide_ref[...].astype(BF16)
    for y in range(NY):
        out_ref[y, pl.ds(0, TOPS), :] = jnp.zeros((TOPS, TILE), F32)
    count = meta_ref[CAP]
    for s in range(CAP):
        place = meta_ref[s]
        row, col = place // TCOLS, place % TCOLS
        lanes = pl.ds(pl.multiple_of(row * TILE, TILE), TILE)
        product = jnp.dot(half_ref[:, lanes], tiles_ref[s], preferred_element_type=F32) * TOP_SCALE
        rows = pl.ds(pl.multiple_of((col // NY) * RANK, RANK), RANK)
        out_ref[col % NY, rows, :] += jnp.where(s < count, product, 0.0)
    half = half_ref[...]
    gram = lax.dot_general(half, half, CONTRACT_LAST, preferred_element_type=F32) * GRAM_SCALE
    packed = jnp.concatenate([gram[16 * i : 16 * i + 16, :] for i in range(4)], axis=1)
    for y in range(NY):
        for z in range(NZ):
            c = z * NY + y
            out_ref[y, pl.ds(TOPS + 2 * z, 2), :] = sent_ref[:, pl.ds(c * TILE, TILE)]
        out_ref[y, pl.ds(TOPS + 2 * NZ, 16), :] = packed


def middle_kernel(in_ref, out_ref):
    gram = in_ref[0, pl.ds(TOPS + 2 * NZ, 16), :]
    for y in range(1, NY):
        gram = gram + in_ref[y, pl.ds(TOPS + 2 * NZ, 16), :]
    for z in range(NZ):
        rows = pl.ds(z * RANK, RANK)
        top = in_ref[0, rows, :]
        for y in range(1, NY):
            top = top + in_ref[y, rows, :]
        out_ref[z, pl.ds(0, RANK), :] = top
        for y in range(NY):
            out_ref[z, pl.ds(RANK + 2 * y, 2), :] = in_ref[y, pl.ds(TOPS + 2 * z, 2), :]
        out_ref[z, pl.ds(RANK + OWN, 16), :] = gram


def update_kernel(in_ref, out_ref):
    packed = in_ref[0, pl.ds(RANK + OWN, 16), :]
    top = in_ref[0, pl.ds(0, RANK), :]
    for z in range(1, NZ):
        packed = packed + in_ref[z, pl.ds(RANK + OWN, 16), :]
        top = top + in_ref[z, pl.ds(0, RANK), :]
    packed = packed * (TOP_SCALE / GRAM_SCALE)
    gram = jnp.concatenate([packed[:, RANK * i : RANK * i + RANK] for i in range(4)], axis=0)
    spec = jnp.concatenate([in_ref[z, pl.ds(RANK, OWN), :] for z in range(NZ)], axis=0)
    bottom = jnp.dot(gram, spec.astype(BF16).astype(F32), precision=lax.Precision.HIGHEST, preferred_element_type=F32)
    new = spec * top / bottom
    fresh = new.astype(BF16)
    rest = new - fresh.astype(F32)
    for z in range(NZ):
        out_ref[z, pl.ds(0, RANK), :] = fresh
        out_ref[z, pl.ds(RANK, OWN), :] = rest[OWN * z : OWN * z + OWN, :].astype(BF16)


def spread_kernel(in_ref, out_ref):
    for y in range(NY):
        for z in range(NZ):
            out_ref[y, pl.ds(z * RANK, RANK), :] = in_ref[z, pl.ds(0, RANK), :]
    for z in range(NZ):
        rest = in_ref[z, pl.ds(RANK, OWN), :].astype(F32)
        for y in range(NY):
            out_ref[y, pl.ds(TOPS + 2 * z, 2), :] = rest[2 * y : 2 * y + 2, :].astype(BF16)


def load_kernel(meta_ref, fresh_ref, tiles_ref, out_ref, acc_ref):
    acc_ref[...] = jnp.zeros_like(acc_ref)
    count = meta_ref[CAP]
    for s in range(CAP):
        place = meta_ref[s]
        row, col = place // TCOLS, place % TCOLS
        rows = pl.ds(pl.multiple_of((col // NY) * RANK, RANK), RANK)
        block = fresh_ref[col % NY, rows, :]
        product = lax.dot_general(block, tiles_ref[s], CONTRACT_LAST, preferred_element_type=F32)
        lanes = pl.ds(pl.multiple_of(row * TILE, TILE), TILE)
        acc_ref[:, lanes] += jnp.where(s < count, product, 0.0)
    gram = jnp.zeros((RANK, RANK), F32)
    for y in range(NY):
        for z in range(NZ):
            block = fresh_ref[y, pl.ds(z * RANK, RANK), :]
            gram = gram + lax.dot_general(block, block, CONTRACT_LAST, preferred_element_type=F32)
    top = acc_ref[...]
    tail = jnp.concatenate([gram, jnp.zeros((RANK, RANK), F32)], axis=1)
    for m in range(NMASS):
        rows = pl.ds(PER * (m // 2), PER)
        out_ref[m % 2, rows, pl.ds(0, PIXELS)] = top[PER * m : PER * m + PER, :]
        out_ref[m % 2, rows, pl.ds(PIXELS, 128)] = tail[PER * m : PER * m + PER, :]


def encode_kernel(in_ref, out_ref):
    total = in_ref[0] + in_ref[1]

    def exponent(x):
        return jnp.floor(jnp.log2(jnp.maximum(jnp.max(x, axis=1, keepdims=True), 1e-30))) - 13.0

    top, gram = total[:, :PIXELS], total[:, PIXELS : PIXELS + RANK]
    top_exp, gram_exp = exponent(top), exponent(gram)
    top = top * jnp.exp2(-top_exp)
    gram = gram * jnp.exp2(-gram_exp)
    lane = lax.broadcasted_iota(jnp.int32, gram.shape, 1)
    tail = jnp.where(lane == 0, top_exp, jnp.where(lane == 1, gram_exp, 0.0))
    tail = jnp.concatenate([gram, tail], axis=1)
    for m in range(NMASS // 2):
        out_ref[m, :, pl.ds(0, PIXELS)] = top[PER * m : PER * m + PER, :]
        out_ref[m, :, pl.ds(PIXELS, 128)] = tail[PER * m : PER * m + PER, :]


def final_kernel(part_ref, half_ref, loading_ref, out_ref):
    top = jnp.zeros((PER, PIXELS), F32)
    gram = jnp.zeros((PER, RANK), F32)
    for m in range(NMASS // 2):
        tail = part_ref[m, :, pl.ds(PIXELS, 128)]
        top = top + part_ref[m, :, pl.ds(0, PIXELS)] * jnp.exp2(tail[:, RANK : RANK + 1])
        gram = gram + tail[:, :RANK] * jnp.exp2(tail[:, RANK + 1 : RANK + 2])
    high = gram.astype(BF16)
    rest = gram - high.astype(F32)
    middle = rest.astype(BF16)
    low = (rest - middle.astype(F32)).astype(BF16)
    parts = jnp.concatenate([x.astype(F32) for x in (high, middle, low, low)], axis=0).astype(BF16)
    sums = jnp.dot(parts, half_ref[...], preferred_element_type=F32)
    bottom = (sums[2 * PER : 3 * PER] + sums[PER : 2 * PER]) + sums[:PER]
    out_ref[...] = loading_ref[...] * top / bottom


def spectra_kernel(place_ref, recv_ref, spec_ref, out_ref):
    zl, yl = place_ref[0], place_ref[1]
    for z in range(NZ):
        for y in range(NY):
            c = z * NY + y
            own = recv_ref[y, pl.ds(pl.multiple_of(z * RANK + OWN * zl, OWN), OWN), :].astype(F32)
            two = own[0:2, :]
            for k in range(1, NY):
                two = jnp.where(yl == k, own[2 * k : 2 * k + 2, :], two)
            rest = recv_ref[y, pl.ds(TOPS + 2 * z, 2), :].astype(F32)
            cols = pl.ds(c * TILE, TILE)
            spec = spec_ref[:, cols]
            out_ref[:, cols] = (two + rest) * (spec / half_precision(spec))


def near(x):
    return pltpu.with_memory_space_constraint(x, pltpu.VMEM)


def call(body, out, *operands, scratch=(), pinned=True):
    specs = [SMEM if x.dtype == jnp.int32 else VMEM for x in operands]
    return pl.pallas_call(
        body,
        out_shape=out,
        in_specs=specs,
        out_specs=jax.tree.map(lambda _: VMEM, out),
        scratch_shapes=scratch,
        compiler_params=PARAMS,
        name=body.__name__,
    )(*[near(x) if pinned and x.dtype != jnp.int32 else x for x in operands])


def local(tiles, tile_pos, kept_tile_count, loading, spectra):
    tiles = tiles[0, 0]
    meta = jnp.concatenate([tile_pos[0, 0], kept_tile_count[0]])

    load = call(own_kernel, pltpu.VMEM((NMASS // 2, PER, PIXELS), BF16), loading, pinned=False)
    load = lax.all_to_all(load, ("zh", "x"), 0, 0, tiled=True)
    load = lax.all_gather(load, "core", axis=0, tiled=False)
    tiles, sent = pl.pallas_call(
        fetch_kernel,
        out_shape=(pltpu.VMEM(tiles.shape, BF16), pltpu.VMEM(spectra.shape, F32)),
        in_specs=[pl.BlockSpec(memory_space=pl.ANY), VMEM],
        out_specs=(VMEM, VMEM),
        scratch_shapes=[pltpu.SemaphoreType.DMA],
        compiler_params=PARAMS,
        name="fetch_kernel",
    )(tiles, spectra)

    out, half = call(
        spec_kernel,
        (pltpu.VMEM((NY, TOPS + 2 * NZ + 16, TILE), F32), pltpu.VMEM((RANK, PIXELS), BF16)),
        meta, load, tiles, sent,
        scratch=[pltpu.VMEM((RANK, PIXELS), F32)],
    )
    part = lax.all_to_all(out.astype(F16), "q", 0, 0, tiled=True)
    part = call(middle_kernel, pltpu.VMEM((NZ, RANK + OWN + 16, TILE), F32), part.astype(F32))
    part = lax.all_to_all(part.astype(F16), "p", 0, 0, tiled=True)

    fresh = call(update_kernel, pltpu.VMEM((NZ, RANK + OWN, TILE), BF16), part.astype(F32))
    fresh = lax.all_to_all(fresh, "p", 0, 0, tiled=True)
    fresh = call(spread_kernel, pltpu.VMEM((NY, TOPS + 2 * NZ, TILE), BF16), fresh)
    fresh = lax.all_to_all(fresh, "q", 0, 0, tiled=True)

    out = call(
        load_kernel,
        pltpu.VMEM((2, RANK // 2, WIDE), F32),
        meta, fresh, tiles,
        scratch=[pltpu.VMEM((RANK, PIXELS), F32)],
    )
    part = lax.all_to_all(out, "core", 0, 0, tiled=True)
    part = call(encode_kernel, pltpu.VMEM((NMASS // 2, PER, WIDE), F32), part)
    part = lax.all_to_all(part.astype(F16), ("zh", "x"), 0, 0, tiled=True).astype(F32)

    place = jnp.stack([lax.axis_index("p"), lax.axis_index("q")]).astype(jnp.int32)
    spectra_new = call(spectra_kernel, jax.ShapeDtypeStruct(spectra.shape, F32), place, fresh, spectra)
    loading_new = call(final_kernel, jax.ShapeDtypeStruct(loading.shape, F32), part, half, loading)
    return (loading_new, spectra_new)


def solution(mesh):
    fine = Mesh(mesh.devices.reshape(NZ, NY, 2, 4, 2), PIX + MASS)
    return jax.shard_map(
        local,
        mesh=fine,
        in_specs=(P(PIX, MASS, None, None, None), P(PIX, MASS, None), P(PIX, MASS), P(MASS, PIX), P(PIX, MASS)),
        out_specs=(P(MASS, PIX), P(PIX, MASS)),
        check_vma=False,
    )
```
